32 devices in a mesh: gx: 4 (over z), gy: 8 (over y, x, core).
Axes of the slice: x: 2, y: 2, z: 4, core: 2. Of those that a mesh axis runs over, the one named last changes fastest.
Arguments:
- operator_blocks: bfloat16 [256, 6, 256, 256], P(('gx', 'gy')), may hold values from -0.15625 to 0.15625
- local_columns: int32 [256, 2], P(('gx', 'gy')), may hold values from 0 to 7
- remote_columns: int32 [256, 4], P(('gx', 'gy')), may hold values from 8 to 17
- match_slots: int32 [256, 6, 2], P(('gx', 'gy')), may hold values from 0 to 2
- tentative: bfloat16 [256, 2, 256, 256], P(('gx', 'gy')), may hold values from -1.5 to 1.5
- inverse_diagonal: bfloat16 [256, 256, 256], P(('gx', 'gy')), may hold values from -0.375 to 0.375
- peer_sends: int32 [32, 8], P(('gx', 'gy')), may hold values from 0 to 7
- slab_sends: int32 [32, 2], P(('gx', 'gy')), may hold values from 0 to 7
- coarse_slots: int32 [256, 2, 2], P(('gx', 'gy')), may hold values from 0 to 47, as said below
Outputs:
- smoothed: bfloat16 [256, 2, 256, 256], P(('gx', 'gy'))
- coarse_operator: bfloat16 [192, 256, 256], P(('gx', 'gy'))
The draws below stay inside these ranges and needn't reach their ends.
Inputs may be any that keep to these rules, and one draw needn't show every extreme that they name: `match_slots`: the value 2 stands for no matching block. `coarse_slots`: no two partial blocks of one device name the same coarse block; coarse block c of a slab belongs to the device of gy index c // 6.
All inputs are finite; a program needn't handle non-finite values.
Results may differ from the reference program's by a relative error of at most 0.012.
Values may be sent and summed in bfloat16 or wider, within the bound.
A program may use at most 128 MiB of HBM per device.

```python
import jax
import jax.numpy as jnp
from jax import lax

B = 256
R = 8
KL = 2
KO = 4
K = 6
KP = 2
S = 1
H = 1
NB = 256
NEXT = 18
CS = 6
NCOARSE = 192
N_GX = 4
N_GY = 8


def draw_coarse_slots(key, part):
    devices = N_GX * N_GY
    total = N_GY * CS
    per_device = R * KP * KP
    key_bias, key_hot, key_noise, key_order = jax.random.split(key, 4)
    bias = jax.random.randint(key_bias, (N_GX, N_GY), 0, 4)
    hot = jax.random.randint(key_hot, (N_GX,), 0, N_GY)
    bias = jnp.where(jnp.arange(N_GY)[None, :] == hot[:, None], 4, bias)
    slot_ids = jnp.arange(total, dtype=jnp.int32)
    owner = slot_ids // CS
    slab = jnp.arange(devices, dtype=jnp.int32) // N_GY
    weight = bias[slab][:, owner]
    weight = jnp.where(((slot_ids == 0) | (slot_ids == total - 1))[None, :], 5, weight)
    noise = jax.random.randint(key_noise, (devices, total), 0, 65536)
    scores = (weight * 65536 + noise) * total + slot_ids[None, :]
    _, picked = lax.top_k(scores, per_device)
    order_keys = jax.random.randint(key_order, (devices, per_device), 0, 65536) * per_device + jnp.arange(per_device, dtype=jnp.int32)[None, :]
    order = jnp.argsort(order_keys, axis=1, stable=True)
    shuffled = jnp.take_along_axis(picked, order, axis=1)
    return shuffled.astype(jnp.int32).reshape(NB, KP, KP)


def touch_ends(values, stream_key, smallest, largest):
    index_at = [jax.random.randint(jax.random.fold_in(stream_key, axis), (), 0, length) for axis, length in enumerate(values.shape)]
    longest = values.shape.index(max(values.shape))
    neighbour = index_at[:longest] + [(index_at[longest] + 1) % values.shape[longest]] + index_at[longest + 1:]
    return values.at[tuple(index_at)].set(smallest).at[tuple(neighbour)].set(largest)


def levels(own_key, extent, cuts, smallest, high):
    def one(axis_at, blocks):
        heights = jax.random.uniform(jax.random.fold_in(jax.random.fold_in(own_key, 6), axis_at), (blocks,), jnp.float32, smallest / len(cuts), high / len(cuts))
        return jnp.repeat(jnp.exp(heights), extent[axis_at] // blocks).reshape((-1,) + (1,) * (len(extent) - axis_at - 1))

    factor_of = one(*cuts[0])
    for cut in cuts[1:]:
        factor_of = factor_of * one(*cut)
    return factor_of


def gaussian(own_key, shape, scale, bound, cuts=(), kind=jnp.bfloat16):
    factor_of = levels(own_key, shape, cuts, -0.22, 0.18) if cuts else 1.0
    array = jax.random.normal(own_key, shape, jnp.float32) * scale * factor_of
    return jnp.minimum(jnp.maximum(array, -bound), bound).astype(kind)


def setup_inputs(seed: int = 0) -> dict:
    key_of = jax.random.split(jax.random.key(seed), 10)
    return {
        "operator_blocks": gaussian(key_of[0], (NB, K, B, B), (K * B) ** -0.5, 0.15625, ((0, 32),)),
        "local_columns": touch_ends(jax.random.randint(key_of[1], (NB, KL), 0, R), jax.random.fold_in(key_of[1], 1), 0, R - 1).astype(jnp.int32),
        "remote_columns": touch_ends(jax.random.randint(key_of[2], (NB, KO), R, NEXT), jax.random.fold_in(key_of[2], 1), R, NEXT - 1).astype(jnp.int32),
        "match_slots": touch_ends(jax.random.randint(key_of[3], (NB, K, KP), 0, KP + 1), jax.random.fold_in(key_of[3], 1), 0, KP).astype(jnp.int32),
        "tentative": gaussian(key_of[4], (NB, KP, B, B), 0.25, 1.5, ((0, 32),)),
        "inverse_diagonal": gaussian(key_of[5], (NB, B, B), B ** -0.5, 0.375, ((0, 32),)),
        "peer_sends": touch_ends(jax.random.randint(key_of[6], (N_GX * N_GY, N_GY * S), 0, R), jax.random.fold_in(key_of[6], 1), 0, R - 1).astype(jnp.int32),
        "slab_sends": touch_ends(jax.random.randint(key_of[7], (N_GX * N_GY, 2 * H), 0, R), jax.random.fold_in(key_of[7], 1), 0, R - 1).astype(jnp.int32),
        "coarse_slots": draw_coarse_slots(jax.random.fold_in(key_of[9], 71), 0),
    }


def select_blocks(picked, matches):
    selected = []
    for out_block in range(matches.shape[2]):
        chosen = jnp.zeros_like(picked[:, :, 0])
        for in_block in range(picked.shape[2]):
            matched = (matches[:, :, out_block] == in_block)[:, :, None, None]
            chosen = jnp.where(matched, picked[:, :, in_block], chosen)
        selected.append(chosen)
    return jnp.stack(selected, axis=2)


def table_map(peer_sends, slab_sends):
    devices = N_GX * N_GY
    device = jnp.arange(devices, dtype=jnp.int32)
    slab = device // N_GY
    member = device % N_GY
    own_rows = device[:, None] * R + jnp.arange(R, dtype=jnp.int32)[None, :]
    entry = jnp.arange(N_GY * S, dtype=jnp.int32)
    source = slab[:, None] * N_GY + entry[None, :] // S
    position = member[:, None] * S + entry[None, :] % S
    peer_rows = source * R + peer_sends[source, position]
    below = jnp.clip(device - N_GY, 0, devices - 1)
    above = jnp.clip(device + N_GY, 0, devices - 1)
    lower_rows = jnp.where((slab >= 1)[:, None], below[:, None] * R + slab_sends[below, :H], NB)
    upper_rows = jnp.where((slab < N_GX - 1)[:, None], above[:, None] * R + slab_sends[above, H:], NB)
    return jnp.concatenate([own_rows, peer_rows, lower_rows, upper_rows], axis=1).astype(jnp.int32)


def product_rows(padded, blocks, columns, matches):
    picked = padded[columns].astype(jnp.float32)
    chosen = select_blocks(picked, matches)
    return jnp.einsum('rkab,rknbc->rnac', blocks.astype(jnp.float32), chosen, precision=lax.Precision.HIGHEST)


def reference(operator_blocks, local_columns, remote_columns, match_slots, tentative, inverse_diagonal, peer_sends, slab_sends, coarse_slots):
    devices = N_GX * N_GY
    lookup = table_map(peer_sends, slab_sends)
    columns = jnp.concatenate([local_columns, remote_columns], axis=1).astype(jnp.int32)
    owner_device = (jnp.arange(NB, dtype=jnp.int32) // R)[:, None]
    global_columns = lookup[owner_device, columns].astype(jnp.int32)
    blocks_dev = operator_blocks.reshape(devices, R, K, B, B)
    columns_dev = global_columns.reshape(devices, R, K)
    matches_dev = match_slots.reshape(devices, R, K, KP)
    inverse_dev = inverse_diagonal.reshape(devices, R, B, B)
    fine_rows = tentative
    for smooth_pass in range(2):
        padded = jnp.concatenate([fine_rows, jnp.zeros((1, KP, B, B), fine_rows.dtype)], axis=0)

        def smooth_device(inputs):
            blocks, device_columns, matches, inverse, rows = inputs
            image = lax.optimization_barrier(product_rows(padded, blocks, device_columns, matches).astype(jnp.bfloat16))
            update = jnp.einsum('rab,rnbc->rnac', inverse.astype(jnp.float32), image.astype(jnp.float32), precision=lax.Precision.HIGHEST)
            return (rows.astype(jnp.float32) - update).astype(jnp.bfloat16)

        fine_rows = lax.map(smooth_device, (blocks_dev, columns_dev, matches_dev, inverse_dev, fine_rows.reshape(devices, R, KP, B, B))).reshape(NB, KP, B, B)
    padded = jnp.concatenate([fine_rows, jnp.zeros((1, KP, B, B), fine_rows.dtype)], axis=0)
    slots_dev = coarse_slots.reshape(devices, R * KP * KP)

    def accumulate(total, inputs):
        blocks, device_columns, matches, rows, slots, device = inputs
        image = lax.optimization_barrier(product_rows(padded, blocks, device_columns, matches).astype(jnp.bfloat16))
        partial_value = jnp.einsum('rnab,rmac->rnmbc', rows.astype(jnp.float32), image.astype(jnp.float32), precision=lax.Precision.HIGHEST)
        partial_value = lax.optimization_barrier(partial_value.astype(jnp.bfloat16)).astype(jnp.float32).reshape(R * KP * KP, B, B)
        targets = (device // N_GY) * (N_GY * CS) + slots
        return total.at[targets].add(partial_value), None

    start = jnp.zeros((NCOARSE, B, B), jnp.float32)
    total, _ = lax.scan(accumulate, start, (blocks_dev, columns_dev, matches_dev, fine_rows.reshape(devices, R, KP, B, B), slots_dev, jnp.arange(devices, dtype=jnp.int32)))
    return fine_rows, total.astype(jnp.bfloat16)
```

```python
import functools

import jax
import jax.numpy as jnp
from jax import lax
from jax.experimental import pallas as pl
from jax.experimental.pallas import tpu as pltpu
from jax.sharding import PartitionSpec as P

MESH = pl.DeviceIdType.MESH


def gather_order(me, group, owned):
    bits = group.bit_length() - 1
    place = jnp.arange(group, dtype=jnp.int32)
    high = place // (group // 2)
    odd = (high + me) % 2
    other = high
    for step in range(1, bits):
        bit = (place >> (bits - 1 - step)) & 1
        other = other | jnp.where(odd == 0, bit << step, bit << (bits - step))
    owner = me ^ other
    slots = owner[:, None] * owned + jnp.arange(owned, dtype=jnp.int32)[None, :]
    return slots.reshape(-1)


def kernel(
    dims,
    local_ref,
    remote_ref,
    match_ref,
    peer_ref,
    slab_ref,
    inverse_ref,
    operator_hbm,
    tentative_hbm,
    diagonal_hbm,
    smooth_hbm,
    coarse_ref,
    operator,
    diagonal,
    own_a,
    own_b,
    rem_a,
    rem_b,
    send,
    local_sum,
    partial,
    half_send,
    total,
    *rest,
):
    slabs, group, rows, kl, ko, kp, peers, halo, owned = dims
    bits = group.bit_length() - 1
    landed = rest[:bits]
    load_sem, out_sem, send_sem, recv_sem, slab_send_sem, slab_recv_sem, half_send_sem, half_recv_sem = rest[bits:]
    width = operator.shape[-1]
    gx = lax.axis_index("gx")
    me = lax.axis_index("gy")
    has_below = gx > 0
    has_above = gx < slabs - 1
    own_zero = rows * kp
    rem_zero = (group * peers + 2 * halo) * kp
    span = peers * kp
    slab_span = halo * kp
    slab_at = group * span
    send_slab_at = group * span

    load_rows = pltpu.make_async_copy(tentative_hbm, own_a.at[pl.ds(0, own_zero)], load_sem.at[0])
    load_rows.start()
    load_operator = pltpu.make_async_copy(operator_hbm, operator, load_sem.at[1])
    load_operator.start()
    load_diagonal = pltpu.make_async_copy(diagonal_hbm, diagonal, load_sem.at[2])
    load_diagonal.start()

    barrier = pltpu.get_barrier_semaphore()

    def greet(offset, carry):
        pl.semaphore_signal(
            barrier, inc=1, device_id=(gx, (me + offset) % group), device_id_type=MESH
        )
        return carry

    lax.fori_loop(1, group, greet, 0)

    @pl.when(has_below)
    def _():
        pl.semaphore_signal(barrier, inc=1, device_id=(gx - 1, me), device_id_type=MESH)

    @pl.when(has_above)
    def _():
        pl.semaphore_signal(barrier, inc=1, device_id=(gx + 1, me), device_id_type=MESH)

    zero = jnp.zeros((width, width), jnp.bfloat16)
    own_a[own_zero] = zero
    own_b[own_zero] = zero
    rem_a[rem_zero] = zero
    rem_b[rem_zero] = zero
    partial[rows * kp * kp] = zero
    neighbours = jnp.where(has_below, 1, 0) + jnp.where(has_above, 1, 0)
    pl.semaphore_wait(barrier, group - 1 + neighbours)

    load_rows.wait()

    def stage(own, row, buffer, at):
        for n in range(kp):
            buffer[at + n] = own[row * kp + n]

    def peer_copy(step, rem, offset):
        target = (me + offset) % group
        return pltpu.make_async_remote_copy(
            src_ref=send.at[pl.ds(offset * span, span)],
            dst_ref=rem.at[pl.ds(me * span, span)],
            send_sem=send_sem.at[step, offset],
            recv_sem=recv_sem.at[step, offset],
            device_id=(gx, target),
            device_id_type=MESH,
        )

    def slab_copy(step, rem, way):
        return pltpu.make_async_remote_copy(
            src_ref=send.at[pl.ds(send_slab_at + way * slab_span, slab_span)],
            dst_ref=rem.at[pl.ds(slab_at + way * slab_span, slab_span)],
            send_sem=slab_send_sem.at[step, way],
            recv_sem=slab_recv_sem.at[step, way],
            device_id=(gx + 1 - 2 * way, me),
            device_id_type=MESH,
        )

    for step in range(3):
        own, after = (own_a, own_b) if step % 2 == 0 else (own_b, own_a)
        rem = rem_a if step % 2 == 0 else rem_b

        def post(offset, carry):
            target = (me + offset) % group
            for s in range(peers):
                stage(own, peer_ref[0, target * peers + s], send, offset * span + s * kp)
            peer_copy(step, rem, offset).start()
            return carry

        lax.fori_loop(1, group, post, 0)
        for way, present in enumerate((has_above, has_below)):

            @pl.when(present)
            def _():
                for h in range(halo):
                    stage(
                        own,
                        slab_ref[0, way * halo + h],
                        send,
                        send_slab_at + way * slab_span + h * kp,
                    )
                slab_copy(step, rem, way).start()

        for s in range(peers):
            stage(own, peer_ref[0, me * peers + s], rem, me * span + s * kp)

        if step == 0:
            load_operator.wait()
        if step == 2:
            store_rows = pltpu.make_async_copy(own.at[pl.ds(0, own_zero)], smooth_hbm, out_sem)
            store_rows.start()

        def local_row(row, carry):
            for n in range(kp):
                value = None
                for k in range(kl):
                    match = match_ref[row, k * kp + n]
                    at = jnp.where(match == kp, own_zero, local_ref[row, k] * kp + match)
                    term = jnp.dot(operator[row, k], own[at], preferred_element_type=jnp.float32)
                    value = term if value is None else value + term
                local_sum[row * kp + n] = value
            return carry

        lax.fori_loop(0, rows, local_row, 0)
        if step == 0:
            load_diagonal.wait()

        def finish(offset, carry):
            peer_copy(step, rem, offset).wait()
            return carry

        lax.fori_loop(1, group, finish, 0)
        for way, (sends, receives) in enumerate(((has_above, has_below), (has_below, has_above))):

            @pl.when(sends)
            def _():
                slab_copy(step, rem, way).wait_send()

            @pl.when(receives)
            def _():
                slab_copy(step, rem, way).wait_recv()

        def remote_row(row, carry):
            images = []
            for n in range(kp):
                value = local_sum[row * kp + n]
                for k in range(ko):
                    match = match_ref[row, (kl + k) * kp + n]
                    source = jnp.maximum(remote_ref[row, k] - rows, 0)
                    from_below = (source >= group * peers) & (source < group * peers + halo)
                    from_above = source >= group * peers + halo
                    absent = (match == kp) | (from_below & (gx == 0)) | (from_above & (gx == slabs - 1))
                    at = jnp.where(absent, rem_zero, source * kp + match)
                    value += jnp.dot(
                        operator[row, kl + k], rem[at], preferred_element_type=jnp.float32
                    )
                images.append(value.astype(jnp.bfloat16))
            if step < 2:
                for n in range(kp):
                    update = jnp.dot(diagonal[row], images[n], preferred_element_type=jnp.float32)
                    before = own[row * kp + n].astype(jnp.float32)
                    after[row * kp + n] = (before - update).astype(jnp.bfloat16)
            else:
                for n1 in range(kp):
                    left = own[row * kp + n1]
                    for n2 in range(kp):
                        block = lax.dot_general(
                            left,
                            images[n2],
                            (((0,), (0,)), ((), ())),
                            preferred_element_type=jnp.float32,
                        )
                        partial[(row * kp + n1) * kp + n2] = block.astype(jnp.bfloat16)
            return carry

        lax.fori_loop(0, rows, remote_row, 0)

    core = me % 2

    def partner(step):
        def flip(bit):
            return me + bit * (1 - 2 * ((me // bit) % 2))

        if step == 0:
            return flip(1)
        return (1 - core) * flip(1 << step) + core * flip(1 << (bits - step))

    def pieces(length):
        middle = length // 2
        return ((middle, length - middle), (0, middle))

    def half_copy(step, piece, length):
        at, count = pieces(length)[piece]
        source = half_send.at[pl.ds(at, count)] if step == 0 else total.at[pl.ds(length + at, count)]
        return pltpu.make_async_remote_copy(
            src_ref=source,
            dst_ref=landed[step].at[pl.ds(at, count)],
            send_sem=half_send_sem.at[step, piece],
            recv_sem=half_recv_sem.at[step, piece],
            device_id=(gx, partner(step)),
            device_id_type=MESH,
        )

    length = group * owned // 2
    for piece in range(2):
        at, count = pieces(length)[piece]

        def pick(j, carry):
            half_send[at + j] = partial[inverse_ref[length + at + j]]
            return carry

        lax.fori_loop(0, count, pick, 0)
        half_copy(0, piece, length).start()

    for step in range(bits):
        last = step == bits - 1
        for piece in range(2):
            at, count = pieces(length)[piece]
            half_copy(step, piece, length).wait_recv()

            def add(j, carry):
                if step == 0:
                    mine = partial[inverse_ref[at + j]]
                else:
                    mine = total[at + j]
                value = mine.astype(jnp.float32) + landed[step][at + j].astype(jnp.float32)
                if last:
                    coarse_ref[at + j] = value.astype(jnp.bfloat16)
                else:
                    total[at + j] = value.astype(jnp.bfloat16)
                return carry

            lax.fori_loop(0, count, add, 0)
            if piece == 0 and not last:
                for sub in range(2):
                    half_copy(step + 1, sub, length // 2).start()
        length //= 2
    length = group * owned // 2
    for step in range(bits):
        for piece in range(2):
            half_copy(step, piece, length).wait_send()
        length //= 2
    store_rows.wait()


def body(
    operator_blocks,
    local_columns,
    remote_columns,
    match_slots,
    tentative,
    inverse_diagonal,
    peer_sends,
    slab_sends,
    coarse_slots,
):
    slabs = lax.axis_size("gx")
    group = lax.axis_size("gy")
    rows, kp, width = tentative.shape[:3]
    kl, ko = local_columns.shape[1], remote_columns.shape[1]
    peers = peer_sends.shape[1] // group
    halo = slab_sends.shape[1] // 2
    owned = (3 * rows * kp * kp // 2 + group - 1) // group
    bits = group.bit_length() - 1
    count = rows * kp * kp
    dims = (slabs, group, rows, kl, ko, kp, peers, halo, owned)

    slots = gather_order(lax.axis_index("gy"), group, owned)
    named = coarse_slots.reshape(-1)
    which = jnp.arange(count, dtype=jnp.int32) - count
    inverse = count + jnp.sum(
        jnp.where(slots[:, None] == named[None, :], which[None, :], 0), axis=1, dtype=jnp.int32
    )

    def blocks(n, dtype=jnp.bfloat16):
        return pltpu.VMEM((n, width, width), dtype)

    smem = pl.BlockSpec(memory_space=pltpu.SMEM)
    anywhere = pl.BlockSpec(memory_space=pl.ANY)
    half = group * owned // 2
    remote_count = (group * peers + 2 * halo) * kp
    smoothed, coarse = pl.pallas_call(
        functools.partial(kernel, dims),
        out_shape=(
            jax.ShapeDtypeStruct((rows * kp, width, width), jnp.bfloat16),
            jax.ShapeDtypeStruct((owned, width, width), jnp.bfloat16),
        ),
        in_specs=[smem] * 6 + [anywhere] * 3,
        out_specs=(anywhere, pl.BlockSpec(memory_space=pltpu.VMEM)),
        scratch_shapes=[
            pltpu.VMEM(operator_blocks.shape, jnp.bfloat16),
            blocks(rows),
            blocks(rows * kp + 1),
            blocks(rows * kp + 1),
            blocks(remote_count + 1),
            blocks(remote_count + 1),
            blocks(remote_count),
            blocks(rows * kp, jnp.float32),
            blocks(count + 1),
            blocks(half),
            blocks(half),
            *[blocks(half >> step) for step in range(bits)],
            pltpu.SemaphoreType.DMA((3,)),
            pltpu.SemaphoreType.DMA,
            pltpu.SemaphoreType.DMA((3, group)),
            pltpu.SemaphoreType.DMA((3, group)),
            pltpu.SemaphoreType.DMA((3, 2)),
            pltpu.SemaphoreType.DMA((3, 2)),
            pltpu.SemaphoreType.DMA((bits, 2)),
            pltpu.SemaphoreType.DMA((bits, 2)),
        ],
        compiler_params=pltpu.CompilerParams(
            collective_id=0, has_side_effects=True, vmem_limit_bytes=67_000_000
        ),
    )(
        local_columns,
        remote_columns,
        match_slots.reshape(rows, -1),
        peer_sends,
        slab_sends,
        inverse,
        operator_blocks,
        tentative.reshape(rows * kp, width, width),
        inverse_diagonal,
    )
    return smoothed.reshape(tentative.shape), coarse


def solution(mesh):
    placed = (
        P(("gx", "gy"), None, None, None),
        P(("gx", "gy"), None),
        P(("gx", "gy"), None),
        P(("gx", "gy"), None, None),
        P(("gx", "gy"), None, None, None),
        P(("gx", "gy"), None, None),
        P(("gx", "gy"), None),
        P(("gx", "gy"), None),
        P(("gx", "gy"), None, None),
    )
    return jax.shard_map(
        body,
        mesh=mesh,
        in_specs=placed,
        out_specs=(P(("gx", "gy"), None, None, None), P(("gx", "gy"), None, None)),
        check_vma=False,
    )
```

```python
import functools

import jax
import jax.numpy as jnp
from jax import lax
from jax.experimental import pallas as pl
from jax.experimental.pallas import tpu as pltpu
from jax.sharding import PartitionSpec as P

MESH = pl.DeviceIdType.MESH


def gather_order(me, group, owned, shape):
    bits = group.bit_length() - 1
    at = lax.broadcasted_iota(jnp.int32, (group * owned, *shape), 0)
    place = at // owned
    high = place // (group // 2)
    odd = (high + me) % 2
    other = high
    for step in range(1, bits):
        bit = (place >> (bits - 1 - step)) & 1
        other = other | jnp.where(odd == 0, bit << step, bit << (bits - step))
    return (me ^ other) * owned + at % owned


def kernel(
    dims,
    local_ref,
    remote_ref,
    match_ref,
    peer_ref,
    slab_ref,
    inverse_ref,
    operator_hbm,
    tentative_hbm,
    diagonal_hbm,
    smooth_hbm,
    coarse_ref,
    operator,
    diagonal,
    own_a,
    own_b,
    rem_a,
    rem_b,
    rem_c,
    send,
    local_sum,
    partial,
    *rest,
):
    slabs, group, rows, kl, ko, kp, peers, halo, owned = dims
    bits = group.bit_length() - 1
    landed = rest[:bits]
    load_sem, out_sem, send_sem, recv_sem, slab_send_sem, slab_recv_sem, half_send_sem, half_recv_sem = rest[bits:]
    width = operator.shape[-1]
    gx = lax.axis_index("gx")
    me = lax.axis_index("gy")
    has_below = gx > 0
    has_above = gx < slabs - 1
    own_zero = rows * kp
    rem_zero = (group * peers + 2 * halo) * kp
    span = peers * kp
    slab_span = halo * kp
    slab_at = group * span
    send_slab_at = group * span

    load_rows = pltpu.make_async_copy(tentative_hbm, own_a.at[pl.ds(0, own_zero)], load_sem.at[0])
    load_rows.start()
    load_operator = pltpu.make_async_copy(operator_hbm, operator, load_sem.at[1])
    load_operator.start()
    load_diagonal = pltpu.make_async_copy(diagonal_hbm, diagonal, load_sem.at[2])
    load_diagonal.start()

    barrier = pltpu.get_barrier_semaphore()

    def greet(offset, carry):
        pl.semaphore_signal(
            barrier, inc=1, device_id=(gx, (me + offset) % group), device_id_type=MESH
        )
        return carry

    lax.fori_loop(1, group, greet, 0)

    @pl.when(has_below)
    def _():
        pl.semaphore_signal(barrier, inc=1, device_id=(gx - 1, me), device_id_type=MESH)

    @pl.when(has_above)
    def _():
        pl.semaphore_signal(barrier, inc=1, device_id=(gx + 1, me), device_id_type=MESH)

    zero = jnp.zeros((width, width), jnp.bfloat16)
    own_a[own_zero] = zero
    own_b[own_zero] = zero
    rem_a[rem_zero] = zero
    rem_b[rem_zero] = zero
    rem_c[rem_zero] = zero
    partial[rows * kp * kp] = zero
    neighbours = jnp.where(has_below, 1, 0) + jnp.where(has_above, 1, 0)
    pl.semaphore_wait(barrier, group - 1 + neighbours)

    load_rows.wait()

    def stage(own, row, buffer, at):
        for n in range(kp):
            buffer[at + n] = own[row * kp + n]

    def peer_copy(step, rem, offset):
        target = (me + offset) % group
        return pltpu.make_async_remote_copy(
            src_ref=send.at[pl.ds(offset * span, span)],
            dst_ref=rem.at[pl.ds(me * span, span)],
            send_sem=send_sem.at[step, offset],
            recv_sem=recv_sem.at[step, offset],
            device_id=(gx, target),
            device_id_type=MESH,
        )

    def slab_copy(step, rem, way):
        return pltpu.make_async_remote_copy(
            src_ref=send.at[pl.ds(send_slab_at + way * slab_span, slab_span)],
            dst_ref=rem.at[pl.ds(slab_at + way * slab_span, slab_span)],
            send_sem=slab_send_sem.at[step, way],
            recv_sem=slab_recv_sem.at[step, way],
            device_id=(gx + 1 - 2 * way, me),
            device_id_type=MESH,
        )

    rems = (rem_a, rem_b, rem_c)

    def post_rows(step, rows_of):
        rem = rems[step]

        def post(turn, carry):
            offset = 1 + (2 * turn + 1) % (group - 1)
            target = (me + offset) % group
            for p in range(peers):
                values = rows_of(peer_ref[0, target * peers + p])
                for n in range(kp):
                    send[offset * span + p * kp + n] = values[n]
            peer_copy(step, rem, offset).start()
            return carry

        lax.fori_loop(0, group - 1, post, 0)
        for way, present in enumerate((has_above, has_below)):

            @pl.when(present)
            def _():
                for h in range(halo):
                    values = rows_of(slab_ref[0, way * halo + h])
                    for n in range(kp):
                        send[send_slab_at + way * slab_span + h * kp + n] = values[n]
                slab_copy(step, rem, way).start()

    post_rows(0, lambda row: [own_a[row * kp + n] for n in range(kp)])

    for step in range(3):
        own, after = (own_a, own_b) if step % 2 == 0 else (own_b, own_a)
        rem = rems[step]
        for p in range(peers):
            stage(own, peer_ref[0, me * peers + p], rem, me * span + p * kp)

        if step == 0:
            load_operator.wait()
        if step == 2:
            store_rows = pltpu.make_async_copy(own.at[pl.ds(0, own_zero)], smooth_hbm, out_sem)
            store_rows.start()

        def local_row(row, carry):
            for n in range(kp):
                value = None
                for k in range(kl):
                    match = match_ref[k, n, row]
                    at = jnp.where(match == kp, own_zero, local_ref[k, row] * kp + match)
                    term = jnp.dot(operator[row, k], own[at], preferred_element_type=jnp.float32)
                    value = term if value is None else value + term
                local_sum[row * kp + n] = value
            return carry

        lax.fori_loop(0, rows, local_row, 0)
        if step == 0:
            load_diagonal.wait()

        def finish(offset, carry):
            peer_copy(step, rem, offset).wait()
            return carry

        lax.fori_loop(1, group, finish, 0)
        for way, (sends, receives) in enumerate(((has_above, has_below), (has_below, has_above))):

            @pl.when(sends)
            def _():
                slab_copy(step, rem, way).wait_send()

            @pl.when(receives)
            def _():
                slab_copy(step, rem, way).wait_recv()

        def images_of(row):
            images = []
            for n in range(kp):
                value = local_sum[row * kp + n]
                for k in range(ko):
                    match = match_ref[kl + k, n, row]
                    source = jnp.maximum(remote_ref[k, row] - rows, 0)
                    from_below = (source >= group * peers) & (source < group * peers + halo)
                    from_above = source >= group * peers + halo
                    absent = (match == kp) | (from_below & (gx == 0)) | (from_above & (gx == slabs - 1))
                    at = jnp.where(absent, rem_zero, source * kp + match)
                    value += jnp.dot(
                        operator[row, kl + k], rem[at], preferred_element_type=jnp.float32
                    )
                images.append(value.astype(jnp.bfloat16))
            return images

        def smoothed_row(row):
            values = []
            for n, image in enumerate(images_of(row)):
                update = jnp.dot(diagonal[row], image, preferred_element_type=jnp.float32)
                before = own[row * kp + n].astype(jnp.float32)
                values.append((before - update).astype(jnp.bfloat16))
            return values

        def own_row(row, carry):
            for n, value in enumerate(smoothed_row(row)):
                after[row * kp + n] = value
            return carry

        def galerkin_row(row, carry):
            images = images_of(row)
            for n1 in range(kp):
                left = own[row * kp + n1]
                for n2 in range(kp):
                    block = lax.dot_general(
                        left,
                        images[n2],
                        (((0,), (0,)), ((), ())),
                        preferred_element_type=jnp.float32,
                    )
                    partial[(row * kp + n1) * kp + n2] = block.astype(jnp.bfloat16)
            return carry

        if step < 2:
            post_rows(step + 1, smoothed_row)
            lax.fori_loop(0, rows, own_row, 0)
        else:
            lax.fori_loop(0, rows, galerkin_row, 0)

    core = me % 2
    total_at = group * owned // 2

    def partner(step):
        def flip(bit):
            return me + bit * (1 - 2 * ((me // bit) % 2))

        if step == 0:
            return flip(1)
        return (1 - core) * flip(1 << step) + core * flip(1 << (bits - step))

    def pieces(length):
        middle = length // 2
        return ((middle, length - middle), (0, middle))

    def half_copy(step, piece, length):
        at, count = pieces(length)[piece]
        source = rem_a.at[pl.ds(at if step == 0 else total_at + length + at, count)]
        return pltpu.make_async_remote_copy(
            src_ref=source,
            dst_ref=landed[step].at[pl.ds(at, count)],
            send_sem=half_send_sem.at[step, piece],
            recv_sem=half_recv_sem.at[step, piece],
            device_id=(gx, partner(step)),
            device_id_type=MESH,
        )

    length = group * owned // 2
    for piece in range(2):
        at, count = pieces(length)[piece]

        def pick(j, carry):
            rem_a[at + j] = partial[inverse_ref[length + at + j]]
            return carry

        lax.fori_loop(0, count, pick, 0)
        half_copy(0, piece, length).start()

    for step in range(bits):
        last = step == bits - 1
        for piece in range(2):
            at, count = pieces(length)[piece]
            half_copy(step, piece, length).wait_recv()

            def add(j, carry):
                if step == 0:
                    mine = partial[inverse_ref[at + j]]
                else:
                    mine = rem_a[total_at + at + j]
                value = mine.astype(jnp.float32) + landed[step][at + j].astype(jnp.float32)
                if last:
                    coarse_ref[at + j] = value.astype(jnp.bfloat16)
                else:
                    rem_a[total_at + at + j] = value.astype(jnp.bfloat16)
                return carry

            lax.fori_loop(0, count, add, 0)
            if piece == 0 and not last:
                for sub in range(2):
                    half_copy(step + 1, sub, length // 2).start()
        length //= 2
    length = group * owned // 2
    for step in range(bits):
        for piece in range(2):
            half_copy(step, piece, length).wait_send()
        length //= 2
    store_rows.wait()


def body(
    operator_blocks,
    local_columns,
    remote_columns,
    match_slots,
    tentative,
    inverse_diagonal,
    peer_sends,
    slab_sends,
    coarse_slots,
):
    slabs = lax.axis_size("gx")
    group = lax.axis_size("gy")
    rows, kp, width = tentative.shape[:3]
    kl, ko = local_columns.shape[1], remote_columns.shape[1]
    peers = peer_sends.shape[1] // group
    halo = slab_sends.shape[1] // 2
    owned = (3 * rows * kp * kp // 2 + group - 1) // group
    bits = group.bit_length() - 1
    count = rows * kp * kp
    dims = (slabs, group, rows, kl, ko, kp, peers, halo, owned)

    named = coarse_slots.transpose(1, 2, 0)
    slots = gather_order(lax.axis_index("gy"), group, owned, named.shape)
    which = [lax.broadcasted_iota(jnp.int32, slots.shape, axis) for axis in (1, 2, 3)]
    which = (which[2] * kp + which[0]) * kp + which[1] - count
    inverse = count + jnp.sum(
        jnp.where(slots == named[None], which, 0), axis=(1, 2, 3), dtype=jnp.int32
    )

    def blocks(n, dtype=jnp.bfloat16):
        return pltpu.VMEM((n, width, width), dtype)

    smem = pl.BlockSpec(memory_space=pltpu.SMEM)
    anywhere = pl.BlockSpec(memory_space=pl.ANY)
    half = group * owned // 2
    remote_count = (group * peers + 2 * halo) * kp
    smoothed, coarse = pl.pallas_call(
        functools.partial(kernel, dims),
        out_shape=(
            jax.ShapeDtypeStruct((rows * kp, width, width), jnp.bfloat16),
            jax.ShapeDtypeStruct((owned, width, width), jnp.bfloat16),
        ),
        in_specs=[smem] * 6 + [anywhere] * 3,
        out_specs=(anywhere, pl.BlockSpec(memory_space=pltpu.VMEM)),
        scratch_shapes=[
            pltpu.VMEM(operator_blocks.shape, jnp.bfloat16),
            blocks(rows),
            blocks(rows * kp + 1),
            blocks(rows * kp + 1),
            blocks(max(remote_count + 1, 2 * half)),
            blocks(remote_count + 1),
            blocks(remote_count + 1),
            blocks(remote_count),
            blocks(rows * kp, jnp.float32),
            blocks(count + 1),
            *[blocks(half >> step) for step in range(bits)],
            pltpu.SemaphoreType.DMA((3,)),
            pltpu.SemaphoreType.DMA,
            pltpu.SemaphoreType.DMA((3, group)),
            pltpu.SemaphoreType.DMA((3, group)),
            pltpu.SemaphoreType.DMA((3, 2)),
            pltpu.SemaphoreType.DMA((3, 2)),
            pltpu.SemaphoreType.DMA((bits, 2)),
            pltpu.SemaphoreType.DMA((bits, 2)),
        ],
        compiler_params=pltpu.CompilerParams(
            collective_id=0, has_side_effects=True, vmem_limit_bytes=67_000_000
        ),
    )(
        local_columns.T,
        remote_columns.T,
        match_slots.transpose(1, 2, 0),
        peer_sends,
        slab_sends,
        inverse,
        operator_blocks,
        tentative.reshape(rows * kp, width, width),
        inverse_diagonal,
    )
    return smoothed.reshape(tentative.shape), coarse


def solution(mesh):
    placed = (
        P(("gx", "gy"), None, None, None),
        P(("gx", "gy"), None),
        P(("gx", "gy"), None),
        P(("gx", "gy"), None, None),
        P(("gx", "gy"), None, None, None),
        P(("gx", "gy"), None, None),
        P(("gx", "gy"), None),
        P(("gx", "gy"), None),
        P(("gx", "gy"), None, None),
    )
    return jax.shard_map(
        body,
        mesh=mesh,
        in_specs=placed,
        out_specs=(P(("gx", "gy"), None, None, None), P(("gx", "gy"), None, None)),
        check_vma=False,
    )
```

```python
import functools

import jax
import jax.numpy as jnp
from jax import lax
from jax.experimental import pallas as pl
from jax.experimental.pallas import tpu as pltpu
from jax.sharding import PartitionSpec as P

MESH = pl.DeviceIdType.MESH


def gather_order(me, group, owned, shape):
    bits = group.bit_length() - 1
    at = lax.broadcasted_iota(jnp.int32, (group * owned, *shape), 0)
    place = at // owned
    high = place // (group // 2)
    odd = (high + me) % 2
    other = high
    for step in range(1, bits):
        bit = (place >> (bits - 1 - step)) & 1
        other = other | jnp.where(odd == 0, bit << step, bit << (bits - step))
    return (me ^ other) * owned + at % owned


def kernel(
    dims,
    local_ref,
    remote_ref,
    match_ref,
    peer_ref,
    slab_ref,
    inverse_ref,
    operator_hbm,
    tentative_hbm,
    diagonal_hbm,
    smooth_hbm,
    coarse_ref,
    operator,
    diagonal,
    own_a,
    own_b,
    rem_a,
    rem_b,
    rem_c,
    send,
    local_sum,
    image,
    *rest,
):
    slabs, group, rows, kl, ko, kp, peers, halo, owned = dims
    bits = group.bit_length() - 1
    landed = rest[:bits]
    load_sem, out_sem, send_sem, recv_sem, slab_send_sem, slab_recv_sem, half_send_sem, half_recv_sem = rest[bits:]
    width = operator.shape[-1]
    gx = lax.axis_index("gx")
    me = lax.axis_index("gy")
    has_below = gx > 0
    has_above = gx < slabs - 1
    own_zero = rows * kp
    rem_zero = (group * peers + 2 * halo) * kp
    span = peers * kp
    slab_span = halo * kp
    slab_at = group * span
    send_slab_at = group * span

    load_rows = pltpu.make_async_copy(tentative_hbm, own_a.at[pl.ds(0, own_zero)], load_sem.at[0])
    load_rows.start()
    load_operator = pltpu.make_async_copy(operator_hbm, operator, load_sem.at[1])
    load_operator.start()
    load_diagonal = pltpu.make_async_copy(diagonal_hbm, diagonal, load_sem.at[2])
    load_diagonal.start()

    barrier = pltpu.get_barrier_semaphore()

    def greet(offset, carry):
        pl.semaphore_signal(
            barrier, inc=1, device_id=(gx, (me + offset) % group), device_id_type=MESH
        )
        return carry

    lax.fori_loop(1, group, greet, 0)

    @pl.when(has_below)
    def _():
        pl.semaphore_signal(barrier, inc=1, device_id=(gx - 1, me), device_id_type=MESH)

    @pl.when(has_above)
    def _():
        pl.semaphore_signal(barrier, inc=1, device_id=(gx + 1, me), device_id_type=MESH)

    zero = jnp.zeros((width, width), jnp.bfloat16)
    own_a[own_zero] = zero
    own_b[own_zero] = zero
    rem_a[rem_zero] = zero
    rem_b[rem_zero] = zero
    rem_c[rem_zero] = zero
    image[own_zero] = zero
    neighbours = jnp.where(has_below, 1, 0) + jnp.where(has_above, 1, 0)
    pl.semaphore_wait(barrier, group - 1 + neighbours)

    load_rows.wait()

    def stage(own, row, buffer, at):
        for n in range(kp):
            buffer[at + n] = own[row * kp + n]

    def peer_copy(step, rem, offset):
        target = (me + offset) % group
        return pltpu.make_async_remote_copy(
            src_ref=send.at[pl.ds(offset * span, span)],
            dst_ref=rem.at[pl.ds(me * span, span)],
            send_sem=send_sem.at[step, offset],
            recv_sem=recv_sem.at[step, offset],
            device_id=(gx, target),
            device_id_type=MESH,
        )

    def slab_copy(step, rem, way):
        return pltpu.make_async_remote_copy(
            src_ref=send.at[pl.ds(send_slab_at + way * slab_span, slab_span)],
            dst_ref=rem.at[pl.ds(slab_at + way * slab_span, slab_span)],
            send_sem=slab_send_sem.at[step, way],
            recv_sem=slab_recv_sem.at[step, way],
            device_id=(gx + 1 - 2 * way, me),
            device_id_type=MESH,
        )

    rems = (rem_a, rem_b, rem_c)

    def post_rows(step, rows_of):
        rem = rems[step]

        def post(turn, carry):
            offset = 1 + (2 * turn + 1) % (group - 1)
            target = (me + offset) % group
            for p in range(peers):
                values = rows_of(peer_ref[0, target * peers + p])
                for n in range(kp):
                    send[offset * span + p * kp + n] = values[n]
            peer_copy(step, rem, offset).start()
            return carry

        lax.fori_loop(0, group - 1, post, 0)
        for way, present in enumerate((has_above, has_below)):

            @pl.when(present)
            def _():
                for h in range(halo):
                    values = rows_of(slab_ref[0, way * halo + h])
                    for n in range(kp):
                        send[send_slab_at + way * slab_span + h * kp + n] = values[n]
                slab_copy(step, rem, way).start()

    post_rows(0, lambda row: [own_a[row * kp + n] for n in range(kp)])

    for step in range(3):
        own, after = (own_a, own_b) if step % 2 == 0 else (own_b, own_a)
        rem = rems[step]
        for p in range(peers):
            stage(own, peer_ref[0, me * peers + p], rem, me * span + p * kp)

        if step == 0:
            load_operator.wait()
        if step == 2:
            store_rows = pltpu.make_async_copy(own.at[pl.ds(0, own_zero)], smooth_hbm, out_sem)
            store_rows.start()

        def local_row(row, carry):
            for n in range(kp):
                value = None
                for k in range(kl):
                    match = match_ref[k, n, row]
                    at = jnp.where(match == kp, own_zero, local_ref[k, row] * kp + match)
                    term = jnp.dot(operator[row, k], own[at], preferred_element_type=jnp.float32)
                    value = term if value is None else value + term
                local_sum[row * kp + n] = value
            return carry

        lax.fori_loop(0, rows, local_row, 0)
        if step == 0:
            load_diagonal.wait()

        def finish(offset, carry):
            peer_copy(step, rem, offset).wait()
            return carry

        lax.fori_loop(1, group, finish, 0)
        for way, (sends, receives) in enumerate(((has_above, has_below), (has_below, has_above))):

            @pl.when(sends)
            def _():
                slab_copy(step, rem, way).wait_send()

            @pl.when(receives)
            def _():
                slab_copy(step, rem, way).wait_recv()

        def images_of(row):
            images = []
            for n in range(kp):
                value = local_sum[row * kp + n]
                for k in range(ko):
                    match = match_ref[kl + k, n, row]
                    source = jnp.maximum(remote_ref[k, row] - rows, 0)
                    from_below = (source >= group * peers) & (source < group * peers + halo)
                    from_above = source >= group * peers + halo
                    absent = (match == kp) | (from_below & (gx == 0)) | (from_above & (gx == slabs - 1))
                    at = jnp.where(absent, rem_zero, source * kp + match)
                    value += jnp.dot(
                        operator[row, kl + k], rem[at], preferred_element_type=jnp.float32
                    )
                images.append(value.astype(jnp.bfloat16))
            return images

        def smoothed_row(row):
            values = []
            for n, image in enumerate(images_of(row)):
                update = jnp.dot(diagonal[row], image, preferred_element_type=jnp.float32)
                before = own[row * kp + n].astype(jnp.float32)
                values.append((before - update).astype(jnp.bfloat16))
            return values

        def own_row(row, carry):
            for n, value in enumerate(smoothed_row(row)):
                after[row * kp + n] = value
            return carry

        def image_row(row, carry):
            for n, value in enumerate(images_of(row)):
                image[row * kp + n] = value
            return carry

        if step < 2:
            post_rows(step + 1, smoothed_row)
            lax.fori_loop(0, rows, own_row, 0)
        else:
            lax.fori_loop(0, rows, image_row, 0)

    core = me % 2
    total_at = group * owned // 2

    def partner(step):
        def flip(bit):
            return me + bit * (1 - 2 * ((me // bit) % 2))

        if step == 0:
            return flip(1)
        return (1 - core) * flip(1 << step) + core * flip(1 << (bits - step))

    grain = owned // 2 if owned % 2 == 0 else owned
    half = group * owned // 2

    def partial_at(place):
        named = inverse_ref[place]
        block = lax.dot_general(
            own_a[named // kp],
            image[named // (kp * kp) * kp + named % kp],
            (((0,), (0,)), ((), ())),
            preferred_element_type=jnp.float32,
        )
        return block.astype(jnp.bfloat16)

    def half_copy(step, chunk):
        at = chunk * grain
        source = at if step == 0 else total_at + (half >> step) + at
        return pltpu.make_async_remote_copy(
            src_ref=rem_a.at[pl.ds(source, grain)],
            dst_ref=landed[step].at[pl.ds(at, grain)],
            send_sem=half_send_sem.at[step, chunk],
            recv_sem=half_recv_sem.at[step, chunk],
            device_id=(gx, partner(step)),
            device_id_type=MESH,
        )

    def send_chunk(chunk):
        def fill(j, carry):
            rem_a[chunk * grain + j] = partial_at(half + chunk * grain + j)
            return carry

        lax.fori_loop(0, grain, fill, 0)
        half_copy(0, chunk).start()

    def add_chunk(step, chunk):
        last = step == bits - 1
        chunks = (half >> step) // grain
        half_copy(step, chunk).wait_recv()

        def add(j, carry):
            at = chunk * grain + j
            mine = partial_at(at) if step == 0 else rem_a[total_at + at]
            value = mine.astype(jnp.float32) + landed[step][at].astype(jnp.float32)
            if last:
                coarse_ref[at] = value.astype(jnp.bfloat16)
            else:
                rem_a[total_at + at] = value.astype(jnp.bfloat16)
            return carry

        lax.fori_loop(0, grain, add, 0)
        if not last and chunk >= chunks // 2:
            half_copy(step + 1, chunk - chunks // 2).start()

    chunks = half // grain
    for chunk in reversed(range(chunks)):
        send_chunk(chunk)
        if chunk + 1 < chunks:
            add_chunk(0, chunk + 1)
    add_chunk(0, 0)
    for step in range(1, bits):
        for chunk in reversed(range((half >> step) // grain)):
            add_chunk(step, chunk)
    for step in range(bits):
        for chunk in range((half >> step) // grain):
            half_copy(step, chunk).wait_send()
    store_rows.wait()


def body(
    operator_blocks,
    local_columns,
    remote_columns,
    match_slots,
    tentative,
    inverse_diagonal,
    peer_sends,
    slab_sends,
    coarse_slots,
):
    slabs = lax.axis_size("gx")
    group = lax.axis_size("gy")
    rows, kp, width = tentative.shape[:3]
    kl, ko = local_columns.shape[1], remote_columns.shape[1]
    peers = peer_sends.shape[1] // group
    halo = slab_sends.shape[1] // 2
    owned = (3 * rows * kp * kp // 2 + group - 1) // group
    bits = group.bit_length() - 1
    count = rows * kp * kp
    dims = (slabs, group, rows, kl, ko, kp, peers, halo, owned)

    named = coarse_slots.transpose(1, 2, 0)
    slots = gather_order(lax.axis_index("gy"), group, owned, named.shape)
    which = [lax.broadcasted_iota(jnp.int32, slots.shape, axis) for axis in (1, 2, 3)]
    which = (which[2] * kp + which[0]) * kp + which[1] - count
    inverse = count + jnp.sum(
        jnp.where(slots == named[None], which, 0), axis=(1, 2, 3), dtype=jnp.int32
    )

    def blocks(n, dtype=jnp.bfloat16):
        return pltpu.VMEM((n, width, width), dtype)

    smem = pl.BlockSpec(memory_space=pltpu.SMEM)
    anywhere = pl.BlockSpec(memory_space=pl.ANY)
    half = group * owned // 2
    remote_count = (group * peers + 2 * halo) * kp
    smoothed, coarse = pl.pallas_call(
        functools.partial(kernel, dims),
        out_shape=(
            jax.ShapeDtypeStruct((rows * kp, width, width), jnp.bfloat16),
            jax.ShapeDtypeStruct((owned, width, width), jnp.bfloat16),
        ),
        in_specs=[smem] * 6 + [anywhere] * 3,
        out_specs=(anywhere, pl.BlockSpec(memory_space=pltpu.VMEM)),
        scratch_shapes=[
            pltpu.VMEM(operator_blocks.shape, jnp.bfloat16),
            blocks(rows),
            blocks(rows * kp + 1),
            blocks(rows * kp + 1),
            blocks(max(remote_count + 1, 2 * half)),
            blocks(remote_count + 1),
            blocks(remote_count + 1),
            blocks(remote_count),
            blocks(rows * kp, jnp.float32),
            blocks(rows * kp + 1),
            *[blocks(half >> step) for step in range(bits)],
            pltpu.SemaphoreType.DMA((3,)),
            pltpu.SemaphoreType.DMA,
            pltpu.SemaphoreType.DMA((3, group)),
            pltpu.SemaphoreType.DMA((3, group)),
            pltpu.SemaphoreType.DMA((3, 2)),
            pltpu.SemaphoreType.DMA((3, 2)),
            pltpu.SemaphoreType.DMA((bits, group)),
            pltpu.SemaphoreType.DMA((bits, group)),
        ],
        compiler_params=pltpu.CompilerParams(
            collective_id=0, has_side_effects=True, vmem_limit_bytes=67_000_000
        ),
    )(
        local_columns.T,
        remote_columns.T,
        match_slots.transpose(1, 2, 0),
        peer_sends,
        slab_sends,
        inverse,
        operator_blocks,
        tentative.reshape(rows * kp, width, width),
        inverse_diagonal,
    )
    return smoothed.reshape(tentative.shape), coarse


def solution(mesh):
    placed = (
        P(("gx", "gy"), None, None, None),
        P(("gx", "gy"), None),
        P(("gx", "gy"), None),
        P(("gx", "gy"), None, None),
        P(("gx", "gy"), None, None, None),
        P(("gx", "gy"), None, None),
        P(("gx", "gy"), None),
        P(("gx", "gy"), None),
        P(("gx", "gy"), None, None),
    )
    return jax.shard_map(
        body,
        mesh=mesh,
        in_specs=placed,
        out_specs=(P(("gx", "gy"), None, None, None), P(("gx", "gy"), None, None)),
        check_vma=False,
    )
```
